32 devices in a mesh: section: 4 (over y, x), expert: 4 (over z), dp: 2 (over core).
Axes of the slice: x: 2, y: 2, z: 4, core: 2. Of those that a mesh axis runs over, the one named last changes fastest.
Arguments:
- activations: bfloat16 [4, 1024, 4096], P('section', ('dp', 'expert')), parts along dimension 1, may hold values from -6 to 6
- routes: int32 [2, 4, 1024, 2], P(None, 'section', ('dp', 'expert')), parts along dimension 2, may hold values from 0 to 3, all different within a row; in each aligned block of 128 rows (0 to 127, 128 to 255, ..., all dimensions but the last counted through in order) at most 72 rows name the same one
- combine: float32 [2, 4, 1024, 2], P(None, 'section', ('dp', 'expert')), parts along dimension 2, may hold values from 0.2 to 1
- norm_gain: float32 [4, 4096], P('section'), may hold values from 0.5 to 2
- up_weight: bfloat16 [4, 4, 4096, 768], P('section', 'expert'), may hold values from -0.09375 to 0.09375
- down_weight: bfloat16 [4, 4, 768, 4096], P('section', 'expert'), may hold values from -0.21875 to 0.21875
Outputs:
- carried: bfloat16 [4, 1024, 4096], P('section', ('dp', 'expert')), parts along dimension 1
The draws below stay inside these ranges and needn't reach their ends.
There are 2 independent parts, one for each index of `dp`. The reference program is written for one: setup_inputs(seed, part) draws one part's arguments, and reference() takes and returns one part's arrays. A program takes and returns all parts, laid end to end along the dimension named above; an argument that names none is the same for every part. Nothing has to cross between parts.
Inputs may be any that keep to these rules, and one draw needn't show every extreme that they name: `routes`: in each aligned block of 128 rows (the rows of one device) no expert is named by more than 72 pairs; the ids of one row differ.
All inputs are finite; a program needn't handle non-finite values.
Results may differ from the reference program's by a relative error of at most 0.007.
Values may be sent and summed in bfloat16 or wider, within the bound.
A program may use at most 128 MiB of HBM per device.

```python
import math
import jax
import jax.numpy as jnp
import numpy as np
from jax import lax

D = 4096
FE = 768
TOK_DEV = 128
STOPS = 2
TOP = 2
CAP = 72
ROWS = 512
N_SECTION = 4
N_EXPERT = 4


def block_scale(own_key, extent, cuts, least, high):
    factor_of, own = 1.0, jax.random.fold_in(own_key, 6)
    for axis_at, shards_of in cuts:
        steps = jnp.exp(jax.random.uniform(jax.random.fold_in(own, axis_at), (shards_of,), jnp.float32, least / len(cuts), high / len(cuts)))
        factor_of = factor_of * jnp.repeat(steps, extent[axis_at] // shards_of).reshape([-1 if axis == axis_at else 1 for axis in range(len(extent))])
    return factor_of


def deal_out(key, own, number, rows, number_of, top, limit, lean):
    ranking = jax.random.permutation(key, number_of)
    crowded, usual = load_shares(number_of, rows * top, limit, lean, True), load_shares(number_of, rows * top, limit, lean, False)
    places = jnp.arange(number_of)

    def named(tallies, rotation):
        used = int((tallies > 0).sum())
        fixed = max(1, used // 4)
        passed = fixed + (places - fixed + rotation * (used - fixed)) % max(1, number_of - fixed)
        return jnp.zeros((number_of,), jnp.int32).at[ranking[jnp.where(places < fixed, places, passed)]].set(jnp.asarray(tallies, jnp.int32))

    tallies = jnp.where(number % 4 == 0, named(crowded, number // 4), named(usual, number - number // 4 - 1))
    mixed = jax.random.permutation(jax.random.fold_in(own, 3), number_of)
    giver, sink = mixed[0:number_of // 2 * 2:2], mixed[1:number_of // 2 * 2:2]
    slack = jnp.minimum(tallies[giver] - 1, limit - tallies[sink]) // 2
    slack = jnp.where((giver == ranking[0]) | (sink == ranking[0]) | (tallies[sink] == 0), 0, jnp.maximum(slack, 0))
    passed = jax.random.randint(jax.random.fold_in(own, 4), (number_of // 2,), 0, 1 << 20) % (slack + 1)
    tallies = tallies.at[giver].add(-passed).at[sink].add(passed)
    members = jnp.searchsorted(jnp.cumsum(tallies), jnp.arange(rows * top), side="right").astype(jnp.int32)
    grid = members.reshape(top, rows).T
    grid = grid[jax.random.permutation(jax.random.fold_in(own, 1), rows)]
    rotation = jax.random.randint(jax.random.fold_in(own, 2), (rows, 1), 0, top)
    return jnp.take_along_axis(grid, (jnp.arange(top)[None, :] + rotation) % top, axis=1)


def load_shares(count, total, limit, skew, full):
    loads = [(1 << 20) // math.isqrt(grade ** skew) + 1 for grade in range(1, count + 1)]
    largest = limit if full else min(limit, max(-(-total // count), total * loads[0] // sum(loads)))
    least = 1 if total - largest >= count - 1 else 0
    counts, rest = [largest] + [least] * (count - 1), total - largest - least * (count - 1)
    while rest > 0:
        candidates = [i for i in range(1, count) if counts[i] < largest] or [i for i in range(1, count) if counts[i] < limit]
        mass, budget = sum([loads[i] for i in candidates]), rest
        for i in candidates:
            extra = min(limit - counts[i], max(1, budget * loads[i] // mass), rest)
            counts[i] = counts[i] + extra
            rest = rest - extra
    return np.array(counts)


def centred(rng, dims, scale, limit, cuts=(), held_as=jnp.bfloat16):
    values = jax.random.normal(rng, dims, jnp.float32) * scale
    if len(cuts) > 0:
        values = block_scale(rng, dims, cuts, -0.22, 0.18) * values
    return jnp.clip(values, min=-limit, max=limit).astype(held_as)


def setup_inputs(seed: int = 0, part: int = 0) -> dict:
    keys = jax.random.split(jax.random.key(seed), 7)
    part_keys = jax.random.split(jax.random.fold_in(keys[6], part), 7)
    activations = centred(part_keys[0], (N_SECTION, ROWS, D), 1.0, 6.0, ((0, 4), (1, 4)))
    routes_keys = jax.random.split(jax.random.fold_in(part_keys[1], 1), STOPS * N_SECTION * ROWS // TOK_DEV)
    routes_turns = jax.random.permutation(jax.random.fold_in(part_keys[1], 3), STOPS * N_SECTION * ROWS // TOK_DEV)
    routes = jax.vmap(lambda own, number: deal_out(jax.random.fold_in(part_keys[1], 2), own, number, TOK_DEV, N_EXPERT, TOP, CAP, 2))(routes_keys, routes_turns).reshape((STOPS, N_SECTION, ROWS, TOP))
    combine = jnp.clip(0.2 + 0.8 * jax.random.uniform(part_keys[2], (STOPS, N_SECTION, ROWS, TOP), jnp.float32) ** block_scale(part_keys[2], (STOPS, N_SECTION, ROWS, TOP), ((1, 4), (2, 4)), -0.2, 0.2), 0.2, 1.0)
    norm_gain = jnp.clip(jnp.exp(math.log(2.0) - 1.3862944 * jax.random.uniform(keys[3], (N_SECTION, D), jnp.float32) ** block_scale(keys[3], (N_SECTION, D), ((0, 4),), -0.2, 0.2)), 0.5, 2.0)
    up_weight = centred(keys[4], (N_SECTION, N_EXPERT, D, FE), D ** -0.5, 0.09375, ((0, 4), (1, 4)))
    down_weight = centred(keys[5], (N_SECTION, N_EXPERT, FE, D), FE ** -0.5, 0.21875, ((0, 4), (1, 4)))
    return dict(activations=activations, routes=routes, combine=combine, norm_gain=norm_gain, up_weight=up_weight, down_weight=down_weight)


def slot_of(expert_ids):
    flattened = expert_ids.reshape(-1)
    onehot = (flattened[:, None] == jnp.arange(N_EXPERT, dtype=jnp.int32)[None, :]).astype(jnp.int32)
    before = jnp.cumsum(onehot, axis=0) - onehot
    return lax.optimization_barrier(jnp.sum(before * onehot, axis=1)).astype(jnp.int32).reshape(expert_ids.shape)

def section_stop(inputs):
    state, expert_ids, weights_now, gain_row, up_proj, down_proj = inputs
    wide_state = state.astype(jnp.float32)
    normed = (wide_state * lax.rsqrt(lax.optimization_barrier(jnp.mean(wide_state * wide_state, axis=-1, keepdims=True)) + 1e-06) * gain_row).astype(jnp.bfloat16)
    blocks = N_EXPERT
    block_ids = expert_ids.reshape(blocks, TOK_DEV, TOP)
    slots = jax.vmap(slot_of)(block_ids)
    block_rows = normed.reshape(blocks, TOK_DEV, D)
    block_index = jnp.arange(blocks, dtype=jnp.int32)[:, None, None]
    spread = jnp.broadcast_to(block_rows[:, :, None, :], (blocks, TOK_DEV, TOP, D))
    outbox = jnp.zeros((blocks, N_EXPERT, CAP, D), jnp.bfloat16).at[block_index, block_ids, slots].set(spread)

    def run_expert(args):
        arrived, up_one, down_one = args
        hidden = jax.nn.silu(jnp.dot(arrived.reshape(-1, D), up_one, preferred_element_type=jnp.float32)).astype(jnp.bfloat16)
        return jnp.dot(hidden, down_one, preferred_element_type=jnp.float32).astype(jnp.bfloat16).reshape(blocks, CAP, D)
    served = lax.map(run_expert, (jnp.transpose(outbox, (1, 0, 2, 3)), up_proj, down_proj))
    picked = served[block_ids, block_index, slots].astype(jnp.float32)
    summed = lax.optimization_barrier(jnp.sum(picked * weights_now.reshape(blocks, TOK_DEV, TOP)[..., None], axis=2))
    return (wide_state + summed.reshape(-1, D)).astype(jnp.bfloat16)

def reference(activations, routes, combine, norm_gain, up_weight, down_weight):
    state = activations
    for visit in range(STOPS):
        mixed = lax.map(section_stop, (state, routes[visit], combine[visit], norm_gain, up_weight, down_weight))
        state = jnp.roll(mixed, 1, axis=0)
    return state
```

```python
import functools

import jax
import jax.numpy as jnp
from jax import lax
from jax.experimental import pallas as pl
from jax.experimental.pallas import tpu as pltpu
from jax.sharding import PartitionSpec as P

MESH = pl.DeviceIdType.MESH
VMEM_ROOM = 56 << 20


def from_behind(value, axis, steps):
    count = lax.axis_size(axis)
    pairs = [(source, (source + steps) % count) for source in range(count)]
    return lax.ppermute(value, axis, pairs)


def tables(routes, combine, experts, capacity):
    tok_rows = routes.shape[1]
    names = jnp.arange(experts, dtype=jnp.int32)
    chosen = (routes[..., None] == names).astype(jnp.float32)
    named = jnp.sum(chosen, axis=2)
    weight = jnp.sum(chosen * combine[..., None], axis=2)
    earlier = jnp.tril(jnp.ones((tok_rows, tok_rows), jnp.float32), -1)
    before = jnp.einsum("rq,vqe->vre", earlier, named, preferred_element_type=jnp.float32)
    slot = jnp.where(named > 0, before, -1.0)
    places = jnp.arange(capacity, dtype=jnp.float32)
    turned = jnp.swapaxes(slot, 1, 2)
    pick = (turned[:, :, None, :] == places[None, None, :, None]).astype(jnp.bfloat16)
    bring = jnp.where(slot[..., None] == places, weight[..., None], 0.0)
    high = lax.reduce_precision(bring, 8, 7)
    low = bring - high
    stops = routes.shape[0]
    slots = experts * capacity
    both = jnp.stack([high, low], axis=1).astype(jnp.bfloat16)
    return pick.reshape(stops, slots, tok_rows), both.reshape(stops, 2, tok_rows, slots)


def relay_kernel(
    stops, experts, sections, capacity, step,
    state_ref, pick_ref, bring_ref, gain_ref, up_hbm, down_hbm, out_ref,
    up_ref, down_ref, later, mixbox, outbox, inbox, servebox, retbox, total, hidden, square,
    weight_sem, send_out, recv_out, send_ret, recv_ret, send_sec, recv_sec,
):
    me = lax.axis_index("expert")
    here = lax.axis_index("section")
    ahead, behind = lax.rem(here + 1, sections), lax.rem(here + sections - 1, sections)
    tok_rows, width = state_ref.shape
    chunks = width // step
    slots = experts * capacity

    fetch_up = pltpu.make_async_copy(up_hbm, up_ref, weight_sem.at[0])
    fetch_down = pltpu.make_async_copy(down_hbm, down_ref, weight_sem.at[1])
    fetch_up.start()
    fetch_down.start()

    barrier = pltpu.get_barrier_semaphore()
    for apart in range(1, experts):
        peer = lax.rem(me + apart, experts)
        pl.semaphore_signal(barrier, inc=1, device_id={"expert": peer}, device_id_type=MESH)
    for peer in (ahead, behind):
        pl.semaphore_signal(barrier, inc=1, device_id={"section": peer}, device_id_type=MESH)
    pl.semaphore_wait(barrier, experts + 1)

    def cols(k):
        return pl.ds(pl.multiple_of(k * step, step), step)

    def over_expert(source, target, send, recv, visit, apart, k):
        peer = lax.rem(me + apart, experts)
        return pltpu.make_async_remote_copy(
            src_ref=source.at[visit, peer, :, cols(k)],
            dst_ref=target.at[visit, me, :, cols(k)],
            send_sem=send.at[visit, apart - 1, k],
            recv_sem=recv.at[visit, apart - 1, k],
            device_id={"expert": peer},
            device_id_type=MESH,
        )

    def dispatch_copy(visit, apart, k):
        return over_expert(outbox, inbox, send_out, recv_out, visit, apart, k)

    def return_copy(visit, apart, k):
        return over_expert(servebox, retbox, send_ret, recv_ret, visit, apart, k)

    def section_copy(visit, k):
        target = out_ref if visit == stops - 1 else later.at[visit]
        return pltpu.make_async_remote_copy(
            src_ref=mixbox.at[visit, :, cols(k)],
            dst_ref=target.at[:, cols(k)],
            send_sem=send_sec.at[visit, k],
            recv_sem=recv_sec.at[visit, k],
            device_id={"section": ahead},
            device_id_type=MESH,
        )

    def state_of(visit):
        return state_ref if visit == 0 else later.at[visit - 1]

    def dispatch(visit, k):
        block = state_of(visit)[:, cols(k)]
        rows = jnp.dot(pick_ref[visit], block, preferred_element_type=jnp.float32)
        rows = rows.reshape(experts, capacity, step).astype(jnp.bfloat16)
        outbox[visit, :, :, cols(k)] = rows
        for apart in range(1, experts):
            dispatch_copy(visit, apart, k).start()
        inbox[visit, me, :, cols(k)] = outbox[visit, me, :, cols(k)]

    def expand(visit, k):
        for apart in range(1, experts):
            dispatch_copy(visit, apart, k).wait_recv()
        rows = inbox[visit, :, :, cols(k)].astype(jnp.float32).reshape(slots, step)
        square[...] += jnp.sum(rows * rows, axis=1, keepdims=True)
        scaled = (rows * gain_ref[:, cols(k)]).astype(jnp.bfloat16)
        total[...] += jnp.dot(scaled, up_ref[cols(k), :], preferred_element_type=jnp.float32)

    def serve(visit, k):
        rows = jnp.dot(hidden[...], down_ref[:, cols(k)], preferred_element_type=jnp.float32)
        rows = rows.reshape(experts, capacity, step).astype(jnp.bfloat16)
        servebox[visit, :, :, cols(k)] = rows
        for apart in range(1, experts):
            return_copy(visit, apart, k).start()
        retbox[visit, me, :, cols(k)] = servebox[visit, me, :, cols(k)]

    def mix(visit, k):
        for apart in range(1, experts):
            return_copy(visit, apart, k).wait_recv()
        rows = retbox[visit, :, :, cols(k)].astype(jnp.float32).reshape(slots, step)
        rows = rows.astype(jnp.bfloat16)
        added = jnp.dot(bring_ref[visit, 0], rows, preferred_element_type=jnp.float32)
        added += jnp.dot(bring_ref[visit, 1], rows, preferred_element_type=jnp.float32)
        wide = state_of(visit)[:, cols(k)].astype(jnp.float32)
        mixbox[visit, :, cols(k)] = (wide + added).astype(jnp.bfloat16)
        section_copy(visit, k).start()

    def each(first, work):
        def turn(k, carry):
            work(k)
            return carry

        lax.fori_loop(first, chunks, turn, 0)

    each(0, lambda k: dispatch(0, k))
    fetch_up.wait()
    for visit in range(stops):
        total[...] = jnp.zeros_like(total)
        square[...] = jnp.zeros_like(square)
        each(0, lambda k: expand(visit, k))
        factor = lax.rsqrt(square[...] * (1.0 / width) + 1e-06)
        before = total[...] * factor
        hidden[...] = (before * jax.nn.sigmoid(before)).astype(jnp.bfloat16)
        if visit == 0:
            fetch_down.wait()
        each(0, lambda k: serve(visit, k))
        if visit < stops - 1:
            mix(visit, 0)

            def both(k):
                mix(visit, k)
                section_copy(visit, k - 1).wait_recv()
                dispatch(visit + 1, k - 1)

            each(1, both)
            section_copy(visit, chunks - 1).wait_recv()
            dispatch(visit + 1, chunks - 1)
        else:
            each(0, lambda k: mix(visit, k))
            each(0, lambda k: section_copy(visit, k).wait_recv())

    for visit in range(stops):

        def drain(k):
            for apart in range(1, experts):
                dispatch_copy(visit, apart, k).wait_send()
                return_copy(visit, apart, k).wait_send()
            section_copy(visit, k).wait_send()

        each(0, drain)


def kernel_body(activations, routes, combine, norm_gain, up_weight, down_weight):
    state = activations[0]
    experts, sections = lax.axis_size("expert"), lax.axis_size("section")
    tok_rows, width = state.shape
    stops, chosen = routes.shape[0], routes.shape[3]
    inner = up_weight.shape[3]
    capacity = tok_rows * chosen // experts * 9 // 8
    slots = experts * capacity
    step = 512 if width % 512 == 0 else width
    chunks = width // step
    pick, bring = tables(routes[:, 0], combine[:, 0], experts, capacity)
    vmem = pl.BlockSpec(memory_space=pltpu.VMEM)
    anywhere = pl.BlockSpec(memory_space=pl.ANY)
    box = pltpu.VMEM((stops, experts, capacity, width), jnp.bfloat16)
    pair = pltpu.SemaphoreType.DMA((stops, experts - 1, chunks))
    line = pltpu.SemaphoreType.DMA((stops, chunks))
    out = pl.pallas_call(
        functools.partial(relay_kernel, stops, experts, sections, capacity, step),
        out_shape=jax.ShapeDtypeStruct((tok_rows, width), jnp.bfloat16),
        in_specs=[vmem] * 4 + [anywhere] * 2,
        out_specs=anywhere,
        scratch_shapes=[
            pltpu.VMEM((width, inner), jnp.bfloat16),
            pltpu.VMEM((inner, width), jnp.bfloat16),
            pltpu.VMEM((max(stops - 1, 1), tok_rows, width), jnp.bfloat16),
            pltpu.VMEM((stops, tok_rows, width), jnp.bfloat16),
            box, box, box, box,
            pltpu.VMEM((slots, inner), jnp.float32),
            pltpu.VMEM((slots, inner), jnp.bfloat16),
            pltpu.VMEM((slots, 1), jnp.float32),
            pltpu.SemaphoreType.DMA((2,)),
            pair, pair, pair, pair, line, line,
        ],
        compiler_params=pltpu.CompilerParams(
            collective_id=0, has_side_effects=True, vmem_limit_bytes=60 << 20
        ),
    )(state, pick, bring, norm_gain, up_weight[0, 0], down_weight[0, 0])
    return out[None]


def slot_of(expert_ids, experts):
    flattened = expert_ids.reshape(-1)
    onehot = (flattened[:, None] == jnp.arange(experts, dtype=jnp.int32)[None, :]).astype(jnp.int32)
    before = jnp.cumsum(onehot, axis=0) - onehot
    return jnp.sum(before * onehot, axis=1).reshape(expert_ids.shape)


def plain_body(activations, routes, combine, norm_gain, up_weight, down_weight):
    state = activations[0]
    gain_row = norm_gain[0]
    up_proj = up_weight[0, 0]
    down_proj = down_weight[0, 0]
    experts = lax.axis_size("expert")
    tok_rows = state.shape[0]
    width = state.shape[1]
    chosen = routes.shape[3]
    capacity = tok_rows * chosen // experts * 9 // 8
    for visit in range(routes.shape[0]):
        expert_ids = routes[visit, 0]
        weights_now = combine[visit, 0]
        wide_state = state.astype(jnp.float32)
        normed = (
            wide_state
            * lax.rsqrt(jnp.mean(wide_state * wide_state, axis=-1, keepdims=True) + 1e-06)
            * gain_row
        ).astype(jnp.bfloat16)
        slots = slot_of(expert_ids, experts)
        spread = jnp.broadcast_to(normed[:, None, :], (tok_rows, chosen, width))
        outbox = (
            jnp.zeros((experts, capacity, width), jnp.bfloat16).at[expert_ids, slots].set(spread)
        )
        arrived = lax.all_to_all(outbox, "expert", split_axis=0, concat_axis=0, tiled=True)
        hidden = jax.nn.silu(
            jnp.dot(arrived.reshape(-1, width), up_proj, preferred_element_type=jnp.float32)
        ).astype(jnp.bfloat16)
        served = (
            jnp.dot(hidden, down_proj, preferred_element_type=jnp.float32)
            .astype(jnp.bfloat16)
            .reshape(arrived.shape)
        )
        returned = lax.all_to_all(served, "expert", split_axis=0, concat_axis=0, tiled=True)
        picked = returned[expert_ids, slots].astype(jnp.float32)
        mixed = (wide_state + jnp.sum(picked * weights_now[..., None], axis=1)).astype(jnp.bfloat16)
        state = from_behind(mixed, "section", 1)
    return state[None]


def body(activations, routes, combine, norm_gain, up_weight, down_weight):
    experts = lax.axis_size("expert")
    tok_rows, width = activations.shape[1:]
    stops, inner = routes.shape[0], up_weight.shape[3]
    capacity = tok_rows * routes.shape[3] // experts * 9 // 8
    boxes = 4 * stops * experts * capacity * width * 2
    rest = 4 * width * inner + (2 * stops + 1) * tok_rows * width * 2 + experts * capacity * inner * 6
    run = kernel_body if boxes + rest <= VMEM_ROOM else plain_body
    return run(activations, routes, combine, norm_gain, up_weight, down_weight)


def solution(mesh):
    placed = (
        P("section", ("dp", "expert"), None),
        P(None, "section", ("dp", "expert"), None),
        P(None, "section", ("dp", "expert"), None),
        P("section", None),
        P("section", "expert", None, None),
        P("section", "expert", None, None),
    )
    return jax.shard_map(
        body,
        mesh=mesh,
        in_specs=placed,
        out_specs=P("section", ("dp", "expert"), None),
        check_vma=False,
    )
```

```python
import functools

import jax
import jax.numpy as jnp
from jax import lax
from jax.experimental import pallas as pl
from jax.experimental.pallas import tpu as pltpu
from jax.sharding import PartitionSpec as P

MESH = pl.DeviceIdType.MESH
VMEM_ROOM = 56 << 20


def from_behind(value, axis, steps):
    count = lax.axis_size(axis)
    pairs = [(source, (source + steps) % count) for source in range(count)]
    return lax.ppermute(value, axis, pairs)


def tables(routes, combine, experts, capacity):
    stops, tok_rows = routes.shape[:2]
    names = jnp.arange(experts, dtype=jnp.int32)
    chosen = (routes[..., None] == names).astype(jnp.float32)
    named = jnp.sum(chosen, axis=2)
    weight = jnp.sum(chosen * combine[..., None], axis=2)
    earlier = jnp.tril(jnp.ones((tok_rows, tok_rows), jnp.float32), -1)
    before = jnp.einsum("rq,vqe->vre", earlier, named, preferred_element_type=jnp.float32)
    slot = jnp.where(named > 0, before, -1.0)
    places = jnp.arange(capacity, dtype=jnp.float32)
    turned = jnp.swapaxes(slot, 1, 2)
    turned_weight = jnp.swapaxes(weight, 1, 2)
    pick = (turned[:, :, None, :] == places[None, None, :, None]).astype(jnp.bfloat16)
    half = experts // 2
    bring = jnp.where(slot[..., None] == places, weight[..., None], 0.0)
    bring = jnp.swapaxes(bring.reshape(stops, tok_rows, 2, half * capacity), 1, 2)
    high = lax.reduce_precision(bring, 8, 7)
    low = bring - high
    both = jnp.stack([high, low], axis=2).astype(jnp.bfloat16)
    tab = jnp.concatenate(
        [
            turned.reshape(stops, 2, half, tok_rows),
            turned_weight.reshape(stops, 2, half, tok_rows),
            jnp.zeros((stops, 2, 8 - 2 * half, tok_rows), jnp.float32),
        ],
        axis=2,
    )
    return pick.reshape(stops, 2, half * capacity, tok_rows), both, jnp.swapaxes(tab, 0, 1)


def relay_kernel(
    stops, sections, capacity, step, edge, lead, lag,
    state_ref, pick_ref, bring_ref, tab_ref, gain_ref, up_hbm, down_hbm, out_ref,
    up_ref, down_ref, later, mixbox, outbox, inbox, servebox, retbox,
    crossbox, pickbox, gatherbox, partbox, partin, tabbox, far_pick, far_bring,
    total, hidden, square, weight_sem,
    send_out, recv_out, send_ret, recv_ret, send_sec, recv_sec,
    send_cross, recv_cross, send_fwd, send_gather, recv_gather, send_part, recv_part,
    send_tab, recv_tab,
):
    me = lax.axis_index("expert")
    here = lax.axis_index("section")
    ahead, behind = lax.rem(here + 1, sections), lax.rem(here + sections - 1, sections)
    half, mine = me // 2, lax.rem(me, 2)
    partner = 2 * half + 1 - mine
    other = 2 * (1 - half)
    gate = 2 - half
    inner = me == 1 + half
    outer = me == 3 * half
    tok_rows, width = state_ref.shape
    chunks = width // step
    near = 2 * capacity
    last = chunks - edge

    fetch_up = pltpu.make_async_copy(up_hbm, up_ref, weight_sem.at[0])
    fetch_down = pltpu.make_async_copy(down_hbm, down_ref, weight_sem.at[1])
    fetch_up.start()
    fetch_down.start()

    barrier = pltpu.get_barrier_semaphore()
    for apart in range(1, 4):
        peer = lax.rem(me + apart, 4)
        pl.semaphore_signal(barrier, inc=1, device_id={"expert": peer}, device_id_type=MESH)
    for peer in (ahead, behind):
        pl.semaphore_signal(barrier, inc=1, device_id={"section": peer}, device_id_type=MESH)
    pl.semaphore_wait(barrier, 5)

    def cols(k):
        return pl.ds(pl.multiple_of(k * step, step), step)

    def send(source, target, send_sem, recv_sem, peer):
        return pltpu.make_async_remote_copy(
            src_ref=source, dst_ref=target, send_sem=send_sem, recv_sem=recv_sem,
            device_id={"expert": peer}, device_id_type=MESH,
        )

    def when(condition):
        return pl.when(condition)

    def tab_copy(place):
        return send(tab_ref.at[1 - half], tabbox.at[place], send_tab, recv_tab.at[place], gate)

    def out_copy(v, k, peer, block):
        return send(outbox.at[v, peer, :, cols(k)], inbox.at[v, block, :, cols(k)],
                    send_out.at[v, peer, k], recv_out.at[v, block, k], peer)

    def cross_copy(v, k, place):
        return send(state_of(v).at[:, cols(k)], crossbox.at[v, place, :, cols(k)],
                    send_cross.at[v, k], recv_cross.at[v, place, k], gate)

    def forward_copy(v, k, q):
        return send(pickbox.at[v, q, 1 - mine, :, cols(k)], inbox.at[v, other + q, :, cols(k)],
                    send_fwd.at[v, q, k], recv_out.at[v, other + q, k], partner)

    def ret_copy(v, k, peer, expert):
        return send(servebox.at[v, peer, :, cols(k)], retbox.at[v, expert, :, cols(k)],
                    send_ret.at[v, peer, k], recv_ret.at[v, expert, k], peer)

    def gather_copy(v, k, q, place):
        return send(servebox.at[v, other + q, :, cols(k)], gatherbox.at[v, q, place, :, cols(k)],
                    send_gather.at[v, q, k], recv_gather.at[v, q, k], partner)

    def part_copy(v, k, q):
        return send(partbox.at[v, q, :, cols(k)], partin.at[v, :, cols(k)],
                    send_part.at[v, q, k], recv_part.at[v, k], other + q)

    def section_copy(v, k):
        target = out_ref if v == stops - 1 else later.at[v]
        return pltpu.make_async_remote_copy(
            src_ref=mixbox.at[v, :, cols(k)], dst_ref=target.at[:, cols(k)],
            send_sem=send_sec.at[v, k], recv_sem=recv_sec.at[v, k],
            device_id={"section": ahead}, device_id_type=MESH,
        )

    def state_of(v):
        return state_ref if v == 0 else later.at[v - 1]

    def dispatch(v, k):
        @when(k < last)
        def _():
            cross_copy(v, k, mine).start()

        block = state_of(v)[:, cols(k)]
        rows = jnp.dot(pick_ref[v, half], block, preferred_element_type=jnp.float32)
        outbox[v, pl.ds(2 * half, 2), :, cols(k)] = rows.reshape(2, capacity, step).astype(jnp.bfloat16)

        @when(k >= last)
        def _():
            far = jnp.dot(pick_ref[v, 1 - half], block, preferred_element_type=jnp.float32)
            outbox[v, pl.ds(other, 2), :, cols(k)] = far.reshape(2, capacity, step).astype(jnp.bfloat16)
            for q in range(2):
                out_copy(v, k, other + q, me).start()

        out_copy(v, k, partner, me).start()
        inbox[v, me, :, cols(k)] = outbox[v, me, :, cols(k)]

    def pass_on(v, k):
        @when(inner)
        def _():
            for q in range(2):
                cross_copy(v, k, q).wait_recv()
                rows = jnp.dot(far_pick[v, q], crossbox[v, q, :, cols(k)], preferred_element_type=jnp.float32)
                pickbox[v, q, :, :, cols(k)] = rows.reshape(2, capacity, step).astype(jnp.bfloat16)
                forward_copy(v, k, q).start()
                inbox[v, other + q, :, cols(k)] = pickbox[v, q, mine, :, cols(k)]

    def expand(v, k):
        out_copy(v, k, partner, partner).wait_recv()

        @when(jnp.logical_or(outer, k >= last))
        def _():
            for q in range(2):
                out_copy(v, k, partner, other + q).wait_recv()

        rows = inbox[v, :, :, cols(k)].astype(jnp.float32).reshape(2 * near, step)
        square[...] += jnp.sum(rows * rows, axis=1, keepdims=True)
        scaled = (rows * gain_ref[:, cols(k)]).astype(jnp.bfloat16)
        total[...] += jnp.dot(scaled, up_ref[cols(k), :], preferred_element_type=jnp.float32)

    def serve(v, k):
        rows = jnp.dot(hidden[...], down_ref[:, cols(k)], preferred_element_type=jnp.float32)
        servebox[v, :, :, cols(k)] = rows.reshape(4, capacity, step).astype(jnp.bfloat16)

        @when(k < edge)
        def _():
            for q in range(2):
                ret_copy(v, k, other + q, me).start()

        @when(jnp.logical_and(outer, k >= edge))
        def _():
            for q in range(2):
                gather_copy(v, k, q, mine).start()

        ret_copy(v, k, partner, me).start()

        @when(jnp.logical_and(inner, k >= edge))
        def _():
            for q in range(2):
                gatherbox[v, q, mine, :, cols(k)] = servebox[v, other + q, :, cols(k)]

        retbox[v, me, :, cols(k)] = servebox[v, me, :, cols(k)]

    def narrow(rows):
        return rows.astype(jnp.float32).reshape(near, step).astype(jnp.bfloat16)

    def combine(v, k):
        @when(inner)
        def _():
            for q in range(2):
                gather_copy(v, k, q, 1 - mine).wait_recv()
                rows = narrow(gatherbox[v, q, :, :, cols(k)])
                part = jnp.dot(far_bring[v, q, 0], rows, preferred_element_type=jnp.float32)
                part += jnp.dot(far_bring[v, q, 1], rows, preferred_element_type=jnp.float32)
                partbox[v, q, :, cols(k)] = part.astype(jnp.bfloat16)
                part_copy(v, k, q).start()

    def mix(v, k):
        ret_copy(v, k, partner, partner).wait_recv()
        rows = narrow(retbox[v, pl.ds(2 * half, 2), :, cols(k)])
        added = jnp.dot(bring_ref[v, half, 0], rows, preferred_element_type=jnp.float32)
        added += jnp.dot(bring_ref[v, half, 1], rows, preferred_element_type=jnp.float32)
        wide = state_of(v)[:, cols(k)].astype(jnp.float32) + added

        @when(k < edge)
        def _():
            for q in range(2):
                ret_copy(v, k, partner, other + q).wait_recv()
            far = narrow(retbox[v, pl.ds(other, 2), :, cols(k)])
            more = jnp.dot(bring_ref[v, 1 - half, 0], far, preferred_element_type=jnp.float32)
            more += jnp.dot(bring_ref[v, 1 - half, 1], far, preferred_element_type=jnp.float32)
            mixbox[v, :, cols(k)] = (wide + more).astype(jnp.bfloat16)

        @when(k >= edge)
        def _():
            part_copy(v, k, 0).wait_recv()
            more = partin[v, :, cols(k)].astype(jnp.float32)
            mixbox[v, :, cols(k)] = (wide + more).astype(jnp.bfloat16)

        section_copy(v, k).start()

    def far_tables(q):
        tab_copy(q).wait_recv()
        for v in range(stops):
            tab = tabbox[q, v]
            place = lax.broadcasted_iota(jnp.int32, (capacity, tok_rows), 0).astype(jnp.float32)
            chosen = [tab[j : j + 1] == place for j in range(2)]
            picks = [jnp.where(c, 1.0, 0.0) for c in chosen]
            far_pick[v, q] = jnp.concatenate(picks, axis=0).astype(jnp.bfloat16)
            brings = [jnp.where(c, tab[2 + j : 3 + j], 0.0) for j, c in enumerate(chosen)]
            brings.append(jnp.zeros((-near % tok_rows, tok_rows), jnp.float32))
            turned = jnp.concatenate(brings, axis=0).T[:, :near]
            high = turned.astype(jnp.bfloat16)
            far_bring[v, q, 0] = high
            far_bring[v, q, 1] = (turned - high.astype(jnp.float32)).astype(jnp.bfloat16)

    def each(first, end, work):
        def turn(k, carry):
            work(k)
            return carry

        lax.fori_loop(first, end, turn, 0)

    tab_copy(mine).start()
    each(0, chunks, lambda k: dispatch(0, k))

    @when(inner)
    def _():
        for q in range(2):
            far_tables(q)

    fetch_up.wait()
    passed = 0
    for v in range(stops):
        total[...] = jnp.zeros_like(total)
        square[...] = jnp.zeros_like(square)

        def take(k):
            @when(jnp.logical_and(k >= passed, k < last))
            def _():
                pass_on(v, k)

            expand(v, k)

        each(0, chunks, take)
        factor = lax.rsqrt(square[...] * (1.0 / width) + 1e-06)
        before = total[...] * factor
        hidden[...] = (before * jax.nn.sigmoid(before)).astype(jnp.bfloat16)
        if v == 0:
            fetch_down.wait()
        each(0, chunks, lambda k: serve(v, k))
        each(edge, max(edge, lead), lambda k: combine(v, k))

        def turn(k):
            @when(jnp.logical_and(k + lead >= edge, k + lead < chunks))
            def _():
                combine(v, k + lead)

            mix(v, k)
            if v < stops - 1:

                @when(k >= 1)
                def _():
                    section_copy(v, k - 1).wait_recv()
                    dispatch(v + 1, k - 1)

                @when(jnp.logical_and(k >= lag, k - lag < last))
                def _():
                    pass_on(v + 1, k - lag)

        each(0, chunks, turn)
        if v < stops - 1:
            section_copy(v, chunks - 1).wait_recv()
            dispatch(v + 1, chunks - 1)
            passed = min(chunks - lag, last)
        else:
            each(0, chunks, lambda k: section_copy(v, k).wait_recv())

    for v in range(stops):

        def drain(k):
            out_copy(v, k, partner, me).wait_send()
            ret_copy(v, k, partner, me).wait_send()
            section_copy(v, k).wait_send()

            @when(k < last)
            def _():
                cross_copy(v, k, mine).wait_send()

            @when(jnp.logical_and(inner, k < last))
            def _():
                for q in range(2):
                    forward_copy(v, k, q).wait_send()

            @when(jnp.logical_and(inner, k >= edge))
            def _():
                for q in range(2):
                    part_copy(v, k, q).wait_send()

            @when(jnp.logical_and(outer, k >= edge))
            def _():
                for q in range(2):
                    gather_copy(v, k, q, mine).wait_send()

            @when(k >= last)
            def _():
                for q in range(2):
                    out_copy(v, k, other + q, me).wait_send()

            @when(k < edge)
            def _():
                for q in range(2):
                    ret_copy(v, k, other + q, me).wait_send()

        each(0, chunks, drain)
    tab_copy(mine).wait_send()


def kernel_body(activations, routes, combine, norm_gain, up_weight, down_weight):
    state = activations[0]
    experts, sections = lax.axis_size("expert"), lax.axis_size("section")
    tok_rows, width = state.shape
    stops, chosen = routes.shape[0], routes.shape[3]
    inner = up_weight.shape[3]
    capacity = tok_rows * chosen // experts * 9 // 8
    slots, near = experts * capacity, experts // 2 * capacity
    step = 256 if width % 256 == 0 else width
    chunks = width // step
    pick, bring, tab = tables(routes[:, 0], combine[:, 0], experts, capacity)
    vmem = pl.BlockSpec(memory_space=pltpu.VMEM)
    anywhere = pl.BlockSpec(memory_space=pl.ANY)
    dma = pltpu.SemaphoreType.DMA
    half_rows = (stops, experts // 2, experts // 2, capacity, width)
    box = pltpu.VMEM((stops, experts, capacity, width), jnp.bfloat16)
    whole = pltpu.VMEM((stops, tok_rows, width), jnp.bfloat16)
    twice = pltpu.VMEM((stops, experts // 2, tok_rows, width), jnp.bfloat16)
    by_expert, by_half, line = dma((stops, experts, chunks)), dma((stops, 2, chunks)), dma((stops, chunks))
    out = pl.pallas_call(
        functools.partial(relay_kernel, stops, sections, capacity, step, 2, 3, 3),
        out_shape=jax.ShapeDtypeStruct((tok_rows, width), jnp.bfloat16),
        in_specs=[vmem] * 5 + [anywhere] * 2,
        out_specs=anywhere,
        scratch_shapes=[
            pltpu.VMEM((width, inner), jnp.bfloat16),
            pltpu.VMEM((inner, width), jnp.bfloat16),
            pltpu.VMEM((max(stops - 1, 1), tok_rows, width), jnp.bfloat16),
            whole,
            box, box, box, box,
            twice,
            pltpu.VMEM(half_rows, jnp.bfloat16),
            pltpu.VMEM(half_rows, jnp.bfloat16),
            twice, whole,
            pltpu.VMEM((2, stops, 8, tok_rows), jnp.float32),
            pltpu.VMEM((stops, 2, near, tok_rows), jnp.bfloat16),
            pltpu.VMEM((stops, 2, 2, tok_rows, near), jnp.bfloat16),
            pltpu.VMEM((slots, inner), jnp.float32),
            pltpu.VMEM((slots, inner), jnp.bfloat16),
            pltpu.VMEM((slots, 1), jnp.float32),
            dma((2,)),
            by_expert, by_expert, by_expert, by_expert, line, line,
            line, by_half, by_half, by_half, by_half, by_half, line,
            dma, dma((2,)),
        ],
        compiler_params=pltpu.CompilerParams(
            collective_id=0, has_side_effects=True, vmem_limit_bytes=62 << 20
        ),
    )(state, pick, bring, tab, norm_gain, up_weight[0, 0], down_weight[0, 0])
    return out[None]


def slot_of(expert_ids, experts):
    flattened = expert_ids.reshape(-1)
    onehot = (flattened[:, None] == jnp.arange(experts, dtype=jnp.int32)[None, :]).astype(jnp.int32)
    before = jnp.cumsum(onehot, axis=0) - onehot
    return jnp.sum(before * onehot, axis=1).reshape(expert_ids.shape)


def plain_body(activations, routes, combine, norm_gain, up_weight, down_weight):
    state = activations[0]
    gain_row = norm_gain[0]
    up_proj = up_weight[0, 0]
    down_proj = down_weight[0, 0]
    experts = lax.axis_size("expert")
    tok_rows = state.shape[0]
    width = state.shape[1]
    chosen = routes.shape[3]
    capacity = tok_rows * chosen // experts * 9 // 8
    for visit in range(routes.shape[0]):
        expert_ids = routes[visit, 0]
        weights_now = combine[visit, 0]
        wide_state = state.astype(jnp.float32)
        normed = (
            wide_state
            * lax.rsqrt(jnp.mean(wide_state * wide_state, axis=-1, keepdims=True) + 1e-06)
            * gain_row
        ).astype(jnp.bfloat16)
        slots = slot_of(expert_ids, experts)
        spread = jnp.broadcast_to(normed[:, None, :], (tok_rows, chosen, width))
        outbox = (
            jnp.zeros((experts, capacity, width), jnp.bfloat16).at[expert_ids, slots].set(spread)
        )
        arrived = lax.all_to_all(outbox, "expert", split_axis=0, concat_axis=0, tiled=True)
        hidden = jax.nn.silu(
            jnp.dot(arrived.reshape(-1, width), up_proj, preferred_element_type=jnp.float32)
        ).astype(jnp.bfloat16)
        served = (
            jnp.dot(hidden, down_proj, preferred_element_type=jnp.float32)
            .astype(jnp.bfloat16)
            .reshape(arrived.shape)
        )
        returned = lax.all_to_all(served, "expert", split_axis=0, concat_axis=0, tiled=True)
        picked = returned[expert_ids, slots].astype(jnp.float32)
        mixed = (wide_state + jnp.sum(picked * weights_now[..., None], axis=1)).astype(jnp.bfloat16)
        state = from_behind(mixed, "section", 1)
    return state[None]


def body(activations, routes, combine, norm_gain, up_weight, down_weight):
    experts = lax.axis_size("expert")
    tok_rows, width = activations.shape[1:]
    stops, inner = routes.shape[0], up_weight.shape[3]
    capacity = tok_rows * routes.shape[3] // experts * 9 // 8
    boxes = 6 * stops * experts * capacity * width * 2
    rest = 4 * width * inner + (7 * stops + 1) * tok_rows * width * 2 + experts * capacity * inner * 6
    fits = experts == 4 and boxes + rest <= VMEM_ROOM
    run = kernel_body if fits else plain_body
    return run(activations, routes, combine, norm_gain, up_weight, down_weight)


def solution(mesh):
    placed = (
        P("section", ("dp", "expert"), None),
        P(None, "section", ("dp", "expert"), None),
        P(None, "section", ("dp", "expert"), None),
        P("section", None),
        P("section", "expert", None, None),
        P("section", "expert", None, None),
    )
    return jax.shard_map(
        body,
        mesh=mesh,
        in_specs=placed,
        out_specs=P("section", ("dp", "expert"), None),
        check_vma=False,
    )
```

```python
import functools

import jax
import jax.numpy as jnp
from jax import lax
from jax.experimental import pallas as pl
from jax.experimental.pallas import tpu as pltpu
from jax.sharding import PartitionSpec as P

MESH = pl.DeviceIdType.MESH
VMEM_ROOM = 56 << 20


def from_behind(value, axis, steps):
    count = lax.axis_size(axis)
    pairs = [(source, (source + steps) % count) for source in range(count)]
    return lax.ppermute(value, axis, pairs)


def tables(routes, combine, experts, capacity):
    stops, tok_rows = routes.shape[:2]
    names = jnp.arange(experts, dtype=jnp.int32)
    chosen = (routes[..., None] == names).astype(jnp.float32)
    named = jnp.sum(chosen, axis=2)
    weight = jnp.sum(chosen * combine[..., None], axis=2)
    earlier = jnp.tril(jnp.ones((tok_rows, tok_rows), jnp.float32), -1)
    before = jnp.einsum("rq,vqe->vre", earlier, named, preferred_element_type=jnp.float32)
    slot = jnp.where(named > 0, before, -1.0)
    places = jnp.arange(capacity, dtype=jnp.float32)
    turned = jnp.swapaxes(slot, 1, 2)
    turned_weight = jnp.swapaxes(weight, 1, 2)
    pick = (turned[:, :, None, :] == places[None, None, :, None]).astype(jnp.bfloat16)
    half = experts // 2
    bring = jnp.where(slot[..., None] == places, weight[..., None], 0.0)
    bring = jnp.swapaxes(bring.reshape(stops, tok_rows, 2, half * capacity), 1, 2)
    high = lax.reduce_precision(bring, 8, 7)
    low = bring - high
    both = jnp.stack([high, low], axis=2).astype(jnp.bfloat16)
    tab = jnp.concatenate(
        [
            turned.reshape(stops, 2, half, tok_rows),
            turned_weight.reshape(stops, 2, half, tok_rows),
            jnp.zeros((stops, 2, 8 - 2 * half, tok_rows), jnp.float32),
        ],
        axis=2,
    )
    return pick.reshape(stops, 2, half * capacity, tok_rows), both, jnp.swapaxes(tab, 0, 1)


def relay_kernel(
    stops, sections, capacity, step, edge, early, lead, lag,
    state_ref, pick_ref, bring_ref, tab_ref, gain_ref, up_hbm, down_hbm, out_ref,
    up_ref, down_ref, later, mixbox, outbox, inbox, servebox, retbox,
    crossbox, pickbox, gatherbox, partbox, partin, tabbox, far_pick, far_bring,
    total, hidden, square, weight_sem,
    send_out, recv_out, send_ret, recv_ret, send_sec, recv_sec,
    send_cross, recv_cross, send_fwd, send_gather, recv_gather, send_part, recv_part,
    send_tab, recv_tab,
):
    me = lax.axis_index("expert")
    here = lax.axis_index("section")
    ahead, behind = lax.rem(here + 1, sections), lax.rem(here + sections - 1, sections)
    half, mine = me // 2, lax.rem(me, 2)
    partner = 2 * half + 1 - mine
    other = 2 * (1 - half)
    gate = 2 - half
    inner = me == 1 + half
    outer = me == 3 * half
    tok_rows, width = state_ref.shape
    chunks = width // step
    near = 2 * capacity
    last = chunks - edge

    fetch_up = pltpu.make_async_copy(up_hbm, up_ref, weight_sem.at[0])
    fetch_down = pltpu.make_async_copy(down_hbm, down_ref, weight_sem.at[1])
    fetch_up.start()
    fetch_down.start()

    barrier = pltpu.get_barrier_semaphore()
    for apart in range(1, 4):
        peer = lax.rem(me + apart, 4)
        pl.semaphore_signal(barrier, inc=1, device_id={"expert": peer}, device_id_type=MESH)
    for peer in (ahead, behind):
        pl.semaphore_signal(barrier, inc=1, device_id={"section": peer}, device_id_type=MESH)
    pl.semaphore_wait(barrier, 5)

    def cols(k):
        return pl.ds(pl.multiple_of(k * step, step), step)

    def send(source, target, send_sem, recv_sem, peer):
        return pltpu.make_async_remote_copy(
            src_ref=source, dst_ref=target, send_sem=send_sem, recv_sem=recv_sem,
            device_id={"expert": peer}, device_id_type=MESH,
        )

    def when(condition):
        return pl.when(condition)

    def tab_copy(place):
        return send(tab_ref.at[1 - half], tabbox.at[place], send_tab, recv_tab.at[place], gate)

    def out_copy(v, k, peer, block):
        return send(outbox.at[v, peer, :, cols(k)], inbox.at[v, block, :, cols(k)],
                    send_out.at[v, peer, k], recv_out.at[v, block, k], peer)

    def cross_copy(v, k, place):
        return send(state_of(v).at[:, cols(k)], crossbox.at[v, place, :, cols(k)],
                    send_cross.at[v, k], recv_cross.at[v, place, k], gate)

    def forward_copy(v, k, q):
        return send(pickbox.at[v, q, 1 - mine, :, cols(k)], inbox.at[v, other + q, :, cols(k)],
                    send_fwd.at[v, q, k], recv_out.at[v, other + q, k], partner)

    def ret_copy(v, k, peer, expert):
        return send(servebox.at[v, peer, :, cols(k)], retbox.at[v, expert, :, cols(k)],
                    send_ret.at[v, peer, k], recv_ret.at[v, expert, k], peer)

    def gather_copy(v, k, q, place):
        return send(servebox.at[v, other + q, :, cols(k)], gatherbox.at[v, q, place, :, cols(k)],
                    send_gather.at[v, q, k], recv_gather.at[v, q, k], partner)

    def part_copy(v, k, q):
        return send(partbox.at[v, q, :, cols(k)], partin.at[v, :, cols(k)],
                    send_part.at[v, q, k], recv_part.at[v, k], other + q)

    def section_copy(v, k):
        target = out_ref if v == stops - 1 else later.at[v]
        return pltpu.make_async_remote_copy(
            src_ref=mixbox.at[v, :, cols(k)], dst_ref=target.at[:, cols(k)],
            send_sem=send_sec.at[v, k], recv_sem=recv_sec.at[v, k],
            device_id={"section": ahead}, device_id_type=MESH,
        )

    def state_of(v):
        return state_ref if v == 0 else later.at[v - 1]

    def dispatch(v, k):
        @when(k < last)
        def _():
            cross_copy(v, k, mine).start()

        block = state_of(v)[:, cols(k)]
        rows = jnp.dot(pick_ref[v, half], block, preferred_element_type=jnp.float32)
        outbox[v, pl.ds(2 * half, 2), :, cols(k)] = rows.reshape(2, capacity, step).astype(jnp.bfloat16)

        @when(k >= last)
        def _():
            far = jnp.dot(pick_ref[v, 1 - half], block, preferred_element_type=jnp.float32)
            outbox[v, pl.ds(other, 2), :, cols(k)] = far.reshape(2, capacity, step).astype(jnp.bfloat16)
            for q in range(2):
                out_copy(v, k, other + q, me).start()

        out_copy(v, k, partner, me).start()
        inbox[v, me, :, cols(k)] = outbox[v, me, :, cols(k)]

    def pass_on(v, k):
        @when(inner)
        def _():
            for q in range(2):
                cross_copy(v, k, q).wait_recv()
                rows = jnp.dot(far_pick[v, q], crossbox[v, q, :, cols(k)], preferred_element_type=jnp.float32)
                pickbox[v, q, :, :, cols(k)] = rows.reshape(2, capacity, step).astype(jnp.bfloat16)
                forward_copy(v, k, q).start()
                inbox[v, other + q, :, cols(k)] = pickbox[v, q, mine, :, cols(k)]

    def expand(v, k):
        out_copy(v, k, partner, partner).wait_recv()

        @when(jnp.logical_or(outer, k >= last))
        def _():
            for q in range(2):
                out_copy(v, k, partner, other + q).wait_recv()

        rows = inbox[v, :, :, cols(k)].astype(jnp.float32).reshape(2 * near, step)
        square[...] += jnp.sum(rows * rows, axis=1, keepdims=True)
        scaled = (rows * gain_ref[:, cols(k)]).astype(jnp.bfloat16)
        total[...] += jnp.dot(scaled, up_ref[cols(k), :], preferred_element_type=jnp.float32)

    def serve(v, k):
        rows = jnp.dot(hidden[...], down_ref[:, cols(k)], preferred_element_type=jnp.float32)
        servebox[v, :, :, cols(k)] = rows.reshape(4, capacity, step).astype(jnp.bfloat16)

        @when(k < edge)
        def _():
            for q in range(2):
                ret_copy(v, k, other + q, me).start()

        @when(jnp.logical_and(outer, k >= edge))
        def _():
            for q in range(2):
                gather_copy(v, k, q, mine).start()

        ret_copy(v, k, partner, me).start()

        @when(jnp.logical_and(inner, k >= edge))
        def _():
            for q in range(2):
                gatherbox[v, q, mine, :, cols(k)] = servebox[v, other + q, :, cols(k)]

        retbox[v, me, :, cols(k)] = servebox[v, me, :, cols(k)]

    def narrow(rows):
        return rows.astype(jnp.float32).reshape(near, step).astype(jnp.bfloat16)

    def combine(v, k):
        @when(inner)
        def _():
            for q in range(2):
                gather_copy(v, k, q, 1 - mine).wait_recv()
                rows = narrow(gatherbox[v, q, :, :, cols(k)])
                part = jnp.dot(far_bring[v, q, 0], rows, preferred_element_type=jnp.float32)
                part += jnp.dot(far_bring[v, q, 1], rows, preferred_element_type=jnp.float32)
                partbox[v, q, :, cols(k)] = part.astype(jnp.bfloat16)
                part_copy(v, k, q).start()

    def mix(v, k):
        ret_copy(v, k, partner, partner).wait_recv()
        rows = narrow(retbox[v, pl.ds(2 * half, 2), :, cols(k)])
        added = jnp.dot(bring_ref[v, half, 0], rows, preferred_element_type=jnp.float32)
        added += jnp.dot(bring_ref[v, half, 1], rows, preferred_element_type=jnp.float32)
        wide = state_of(v)[:, cols(k)].astype(jnp.float32) + added

        @when(k < edge)
        def _():
            for q in range(2):
                ret_copy(v, k, partner, other + q).wait_recv()
            far = narrow(retbox[v, pl.ds(other, 2), :, cols(k)])
            more = jnp.dot(bring_ref[v, 1 - half, 0], far, preferred_element_type=jnp.float32)
            more += jnp.dot(bring_ref[v, 1 - half, 1], far, preferred_element_type=jnp.float32)
            mixbox[v, :, cols(k)] = (wide + more).astype(jnp.bfloat16)

        @when(k >= edge)
        def _():
            part_copy(v, k, 0).wait_recv()
            more = partin[v, :, cols(k)].astype(jnp.float32)
            mixbox[v, :, cols(k)] = (wide + more).astype(jnp.bfloat16)

        section_copy(v, k).start()

    def far_tables(q):
        tab_copy(q).wait_recv()
        for v in range(stops):
            tab = tabbox[q, v]
            place = lax.broadcasted_iota(jnp.int32, (capacity, tok_rows), 0).astype(jnp.float32)
            chosen = [tab[j : j + 1] == place for j in range(2)]
            picks = [jnp.where(c, 1.0, 0.0) for c in chosen]
            far_pick[v, q] = jnp.concatenate(picks, axis=0).astype(jnp.bfloat16)
            brings = [jnp.where(c, tab[2 + j : 3 + j], 0.0) for j, c in enumerate(chosen)]
            brings.append(jnp.zeros((-near % tok_rows, tok_rows), jnp.float32))
            turned = jnp.concatenate(brings, axis=0).T[:, :near]
            high = turned.astype(jnp.bfloat16)
            far_bring[v, q, 0] = high
            far_bring[v, q, 1] = (turned - high.astype(jnp.float32)).astype(jnp.bfloat16)

    def each(first, end, work):
        def turn(k, carry):
            work(k)
            return carry

        lax.fori_loop(first, end, turn, 0)

    tab_copy(mine).start()
    each(0, chunks, lambda k: dispatch(0, k))

    @when(inner)
    def _():
        for q in range(2):
            far_tables(q)

    fetch_up.wait()
    passed = 0
    for v in range(stops):
        total[...] = jnp.zeros_like(total)
        square[...] = jnp.zeros_like(square)

        def take(k):
            @when(jnp.logical_and(k >= passed, k < last))
            def _():
                pass_on(v, k)

            expand(v, k)

        each(0, chunks, take)
        factor = lax.rsqrt(square[...] * (1.0 / width) + 1e-06)
        before = total[...] * factor
        hidden[...] = (before * jax.nn.sigmoid(before)).astype(jnp.bfloat16)
        if v == 0:
            fetch_down.wait()
        each(0, jnp.where(outer, chunks, early), lambda k: serve(v, k))
        each(edge, max(edge, lead), lambda k: combine(v, k))

        def turn(k):
            @when(jnp.logical_and(inner, k + early < chunks))
            def _():
                serve(v, k + early)

            @when(jnp.logical_and(k + lead >= edge, k + lead < chunks))
            def _():
                combine(v, k + lead)

            mix(v, k)
            if v < stops - 1:

                @when(k >= 1)
                def _():
                    section_copy(v, k - 1).wait_recv()
                    dispatch(v + 1, k - 1)

                @when(jnp.logical_and(k >= lag, k - lag < last))
                def _():
                    pass_on(v + 1, k - lag)

        each(0, chunks, turn)
        if v < stops - 1:
            section_copy(v, chunks - 1).wait_recv()
            dispatch(v + 1, chunks - 1)
            passed = min(chunks - lag, last)
        else:
            each(0, chunks, lambda k: section_copy(v, k).wait_recv())

    for v in range(stops):

        def drain(k):
            out_copy(v, k, partner, me).wait_send()
            ret_copy(v, k, partner, me).wait_send()
            section_copy(v, k).wait_send()

            @when(k < last)
            def _():
                cross_copy(v, k, mine).wait_send()

            @when(jnp.logical_and(inner, k < last))
            def _():
                for q in range(2):
                    forward_copy(v, k, q).wait_send()

            @when(jnp.logical_and(inner, k >= edge))
            def _():
                for q in range(2):
                    part_copy(v, k, q).wait_send()

            @when(jnp.logical_and(outer, k >= edge))
            def _():
                for q in range(2):
                    gather_copy(v, k, q, mine).wait_send()

            @when(k >= last)
            def _():
                for q in range(2):
                    out_copy(v, k, other + q, me).wait_send()

            @when(k < edge)
            def _():
                for q in range(2):
                    ret_copy(v, k, other + q, me).wait_send()

        each(0, chunks, drain)
    tab_copy(mine).wait_send()


def kernel_body(activations, routes, combine, norm_gain, up_weight, down_weight):
    state = activations[0]
    experts, sections = lax.axis_size("expert"), lax.axis_size("section")
    tok_rows, width = state.shape
    stops, chosen = routes.shape[0], routes.shape[3]
    inner = up_weight.shape[3]
    capacity = tok_rows * chosen // experts * 9 // 8
    slots, near = experts * capacity, experts // 2 * capacity
    step = 256 if width % 256 == 0 else width
    chunks = width // step
    pick, bring, tab = tables(routes[:, 0], combine[:, 0], experts, capacity)
    vmem = pl.BlockSpec(memory_space=pltpu.VMEM)
    anywhere = pl.BlockSpec(memory_space=pl.ANY)
    dma = pltpu.SemaphoreType.DMA
    half_rows = (stops, experts // 2, experts // 2, capacity, width)
    box = pltpu.VMEM((stops, experts, capacity, width), jnp.bfloat16)
    whole = pltpu.VMEM((stops, tok_rows, width), jnp.bfloat16)
    twice = pltpu.VMEM((stops, experts // 2, tok_rows, width), jnp.bfloat16)
    by_expert, by_half, line = dma((stops, experts, chunks)), dma((stops, 2, chunks)), dma((stops, chunks))
    out = pl.pallas_call(
        functools.partial(relay_kernel, stops, sections, capacity, step, 2, 9, 8, 6),
        out_shape=jax.ShapeDtypeStruct((tok_rows, width), jnp.bfloat16),
        in_specs=[vmem] * 5 + [anywhere] * 2,
        out_specs=anywhere,
        scratch_shapes=[
            pltpu.VMEM((width, inner), jnp.bfloat16),
            pltpu.VMEM((inner, width), jnp.bfloat16),
            pltpu.VMEM((max(stops - 1, 1), tok_rows, width), jnp.bfloat16),
            whole,
            box, box, box, box,
            twice,
            pltpu.VMEM(half_rows, jnp.bfloat16),
            pltpu.VMEM(half_rows, jnp.bfloat16),
            twice, whole,
            pltpu.VMEM((2, stops, 8, tok_rows), jnp.float32),
            pltpu.VMEM((stops, 2, near, tok_rows), jnp.bfloat16),
            pltpu.VMEM((stops, 2, 2, tok_rows, near), jnp.bfloat16),
            pltpu.VMEM((slots, inner), jnp.float32),
            pltpu.VMEM((slots, inner), jnp.bfloat16),
            pltpu.VMEM((slots, 1), jnp.float32),
            dma((2,)),
            by_expert, by_expert, by_expert, by_expert, line, line,
            line, by_half, by_half, by_half, by_half, by_half, line,
            dma, dma((2,)),
        ],
        compiler_params=pltpu.CompilerParams(
            collective_id=0, has_side_effects=True, vmem_limit_bytes=62 << 20
        ),
    )(state, pick, bring, tab, norm_gain, up_weight[0, 0], down_weight[0, 0])
    return out[None]


def slot_of(expert_ids, experts):
    flattened = expert_ids.reshape(-1)
    onehot = (flattened[:, None] == jnp.arange(experts, dtype=jnp.int32)[None, :]).astype(jnp.int32)
    before = jnp.cumsum(onehot, axis=0) - onehot
    return jnp.sum(before * onehot, axis=1).reshape(expert_ids.shape)


def plain_body(activations, routes, combine, norm_gain, up_weight, down_weight):
    state = activations[0]
    gain_row = norm_gain[0]
    up_proj = up_weight[0, 0]
    down_proj = down_weight[0, 0]
    experts = lax.axis_size("expert")
    tok_rows = state.shape[0]
    width = state.shape[1]
    chosen = routes.shape[3]
    capacity = tok_rows * chosen // experts * 9 // 8
    for visit in range(routes.shape[0]):
        expert_ids = routes[visit, 0]
        weights_now = combine[visit, 0]
        wide_state = state.astype(jnp.float32)
        normed = (
            wide_state
            * lax.rsqrt(jnp.mean(wide_state * wide_state, axis=-1, keepdims=True) + 1e-06)
            * gain_row
        ).astype(jnp.bfloat16)
        slots = slot_of(expert_ids, experts)
        spread = jnp.broadcast_to(normed[:, None, :], (tok_rows, chosen, width))
        outbox = (
            jnp.zeros((experts, capacity, width), jnp.bfloat16).at[expert_ids, slots].set(spread)
        )
        arrived = lax.all_to_all(outbox, "expert", split_axis=0, concat_axis=0, tiled=True)
        hidden = jax.nn.silu(
            jnp.dot(arrived.reshape(-1, width), up_proj, preferred_element_type=jnp.float32)
        ).astype(jnp.bfloat16)
        served = (
            jnp.dot(hidden, down_proj, preferred_element_type=jnp.float32)
            .astype(jnp.bfloat16)
            .reshape(arrived.shape)
        )
        returned = lax.all_to_all(served, "expert", split_axis=0, concat_axis=0, tiled=True)
        picked = returned[expert_ids, slots].astype(jnp.float32)
        mixed = (wide_state + jnp.sum(picked * weights_now[..., None], axis=1)).astype(jnp.bfloat16)
        state = from_behind(mixed, "section", 1)
    return state[None]


def body(activations, routes, combine, norm_gain, up_weight, down_weight):
    experts = lax.axis_size("expert")
    tok_rows, width = activations.shape[1:]
    stops, inner = routes.shape[0], up_weight.shape[3]
    capacity = tok_rows * routes.shape[3] // experts * 9 // 8
    boxes = 6 * stops * experts * capacity * width * 2
    rest = 4 * width * inner + (7 * stops + 1) * tok_rows * width * 2 + experts * capacity * inner * 6
    fits = experts == 4 and boxes + rest <= VMEM_ROOM
    run = kernel_body if fits else plain_body
    return run(activations, routes, combine, norm_gain, up_weight, down_weight)


def solution(mesh):
    placed = (
        P("section", ("dp", "expert"), None),
        P(None, "section", ("dp", "expert"), None),
        P(None, "section", ("dp", "expert"), None),
        P("section", None),
        P("section", "expert", None, None),
        P("section", "expert", None, None),
    )
    return jax.shard_map(
        body,
        mesh=mesh,
        in_specs=placed,
        out_specs=P("section", ("dp", "expert"), None),
        check_vma=False,
    )
```

```python
import functools

import jax
import jax.numpy as jnp
from jax import lax
from jax.experimental import pallas as pl
from jax.experimental.pallas import tpu as pltpu
from jax.sharding import PartitionSpec as P

MESH = pl.DeviceIdType.MESH
VMEM_ROOM = 56 << 20


def from_behind(value, axis, steps):
    count = lax.axis_size(axis)
    pairs = [(source, (source + steps) % count) for source in range(count)]
    return lax.ppermute(value, axis, pairs)


def tables(routes, combine, experts, capacity):
    stops, tok_rows = routes.shape[:2]
    names = jnp.arange(experts, dtype=jnp.int32)
    chosen = (routes[..., None] == names).astype(jnp.float32)
    named = jnp.sum(chosen, axis=2)
    weight = jnp.sum(chosen * combine[..., None], axis=2)
    earlier = jnp.tril(jnp.ones((tok_rows, tok_rows), jnp.float32), -1)
    before = jnp.einsum("rq,vqe->vre", earlier, named, preferred_element_type=jnp.float32)
    slot = jnp.where(named > 0, before, -1.0)
    places = jnp.arange(capacity, dtype=jnp.float32)
    turned = jnp.swapaxes(slot, 1, 2)
    turned_weight = jnp.swapaxes(weight, 1, 2)
    pick = (turned[:, :, None, :] == places[None, None, :, None]).astype(jnp.bfloat16)
    half = experts // 2
    bring = jnp.where(slot[..., None] == places, weight[..., None], 0.0)
    bring = jnp.swapaxes(bring.reshape(stops, tok_rows, 2, half * capacity), 1, 2)
    high = lax.reduce_precision(bring, 8, 7)
    low = bring - high
    both = jnp.stack([high, low], axis=2).astype(jnp.bfloat16)
    tab = jnp.concatenate(
        [
            turned.reshape(stops, 2, half, tok_rows),
            turned_weight.reshape(stops, 2, half, tok_rows),
            jnp.zeros((stops, 2, 8 - 2 * half, tok_rows), jnp.float32),
        ],
        axis=2,
    )
    return pick.reshape(stops, 2, half * capacity, tok_rows), both, jnp.swapaxes(tab, 0, 1)


def relay_kernel(
    stops, sections, capacity, step, edge, early, lead, lag,
    state_ref, pick_ref, bring_ref, tab_ref, gain_ref, up_hbm, down_hbm, out_ref,
    up_ref, down_ref, later, mixbox, outbox, inbox, servebox, retbox,
    crossbox, pickbox, gatherbox, partbox, partin, tabbox, far_pick, far_bring,
    total, hidden, square, weight_sem,
    send_out, recv_out, send_ret, recv_ret, send_sec, recv_sec,
    send_cross, recv_cross, send_fwd, send_gather, recv_gather, send_part, recv_part,
    send_tab, recv_tab,
):
    me = lax.axis_index("expert")
    here = lax.axis_index("section")
    ahead, behind = lax.rem(here + 1, sections), lax.rem(here + sections - 1, sections)
    half, mine = me // 2, lax.rem(me, 2)
    partner = 2 * half + 1 - mine
    other = 2 * (1 - half)
    gate = 2 - half
    inner = me == 1 + half
    outer = me == 3 * half
    tok_rows, width = state_ref.shape
    chunks = width // step
    near = 2 * capacity
    last = chunks - edge

    fetch_up = pltpu.make_async_copy(up_hbm, up_ref, weight_sem.at[0])
    fetch_down = pltpu.make_async_copy(down_hbm, down_ref, weight_sem.at[1])
    fetch_up.start()
    fetch_down.start()

    barrier = pltpu.get_barrier_semaphore()
    for apart in range(1, 4):
        peer = lax.rem(me + apart, 4)
        pl.semaphore_signal(barrier, inc=1, device_id={"expert": peer}, device_id_type=MESH)
    for peer in (ahead, behind):
        pl.semaphore_signal(barrier, inc=1, device_id={"section": peer}, device_id_type=MESH)
    pl.semaphore_wait(barrier, 5)

    def cols(k):
        return pl.ds(pl.multiple_of(k * step, step), step)

    def send(source, target, send_sem, recv_sem, peer):
        return pltpu.make_async_remote_copy(
            src_ref=source, dst_ref=target, send_sem=send_sem, recv_sem=recv_sem,
            device_id={"expert": peer}, device_id_type=MESH,
        )

    def when(condition):
        return pl.when(condition)

    def tab_copy(place):
        return send(tab_ref.at[1 - half], tabbox.at[place], send_tab, recv_tab.at[place], gate)

    def out_copy(v, k, peer, block):
        return send(outbox.at[v, peer, :, cols(k)], inbox.at[v, block, :, cols(k)],
                    send_out.at[v, peer, k], recv_out.at[v, block, k], peer)

    def cross_copy(v, k, place):
        return send(state_of(v).at[:, cols(k)], crossbox.at[v, place, :, cols(k)],
                    send_cross.at[v, k], recv_cross.at[v, place, k], gate)

    def forward_copy(v, k, q):
        return send(pickbox.at[v, q, 1 - mine, :, cols(k)], inbox.at[v, other + q, :, cols(k)],
                    send_fwd.at[v, q, k], recv_out.at[v, other + q, k], partner)

    def ret_copy(v, k, peer, expert):
        return send(servebox.at[v, peer, :, cols(k)], retbox.at[v, expert, :, cols(k)],
                    send_ret.at[v, peer, k], recv_ret.at[v, expert, k], peer)

    def gather_copy(v, k, q, place):
        return send(servebox.at[v, other + q, :, cols(k)], gatherbox.at[v, q, place, :, cols(k)],
                    send_gather.at[v, q, k], recv_gather.at[v, q, k], partner)

    def part_copy(v, k, q):
        return send(partbox.at[v, q, :, cols(k)], partin.at[v, :, cols(k)],
                    send_part.at[v, q, k], recv_part.at[v, k], other + q)

    def section_copy(v, k):
        target = out_ref if v == stops - 1 else later.at[v]
        return pltpu.make_async_remote_copy(
            src_ref=mixbox.at[v, :, cols(k)], dst_ref=target.at[:, cols(k)],
            send_sem=send_sec.at[v, k], recv_sem=recv_sec.at[v, k],
            device_id={"section": ahead}, device_id_type=MESH,
        )

    def state_of(v):
        return state_ref if v == 0 else later.at[v - 1]

    def dispatch(v, k):
        @when(k < last)
        def _():
            cross_copy(v, k, mine).start()

        block = state_of(v)[:, cols(k)]
        rows = jnp.dot(pick_ref[v, half], block, preferred_element_type=jnp.float32)
        outbox[v, pl.ds(2 * half, 2), :, cols(k)] = rows.reshape(2, capacity, step).astype(jnp.bfloat16)

        @when(k >= last)
        def _():
            far = jnp.dot(pick_ref[v, 1 - half], block, preferred_element_type=jnp.float32)
            outbox[v, pl.ds(other, 2), :, cols(k)] = far.reshape(2, capacity, step).astype(jnp.bfloat16)
            for q in range(2):
                out_copy(v, k, other + q, me).start()

        out_copy(v, k, partner, me).start()
        inbox[v, me, :, cols(k)] = outbox[v, me, :, cols(k)]

    def pass_on(v, k):
        @when(inner)
        def _():
            for q in range(2):
                cross_copy(v, k, q).wait_recv()
                rows = jnp.dot(far_pick[v, q], crossbox[v, q, :, cols(k)], preferred_element_type=jnp.float32)
                pickbox[v, q, :, :, cols(k)] = rows.reshape(2, capacity, step).astype(jnp.bfloat16)
                forward_copy(v, k, q).start()
                inbox[v, other + q, :, cols(k)] = pickbox[v, q, mine, :, cols(k)]

    def expand(v, k):
        out_copy(v, k, partner, partner).wait_recv()

        @when(jnp.logical_or(outer, k >= last))
        def _():
            for q in range(2):
                out_copy(v, k, partner, other + q).wait_recv()

        rows = inbox[v, :, :, cols(k)].astype(jnp.float32).reshape(2 * near, step)
        square[...] += jnp.sum(rows * rows, axis=1, keepdims=True)
        scaled = (rows * gain_ref[:, cols(k)]).astype(jnp.bfloat16)
        total[...] += jnp.dot(scaled, up_ref[cols(k), :], preferred_element_type=jnp.float32)

    def serve(v, k):
        rows = jnp.dot(hidden[...], down_ref[:, cols(k)], preferred_element_type=jnp.float32)
        servebox[v, :, :, cols(k)] = rows.reshape(4, capacity, step).astype(jnp.bfloat16)

        @when(k < edge)
        def _():
            for q in range(2):
                ret_copy(v, k, other + q, me).start()

        @when(jnp.logical_and(outer, k >= edge))
        def _():
            for q in range(2):
                gather_copy(v, k, q, mine).start()

        ret_copy(v, k, partner, me).start()

        @when(jnp.logical_and(inner, k >= edge))
        def _():
            for q in range(2):
                gatherbox[v, q, mine, :, cols(k)] = servebox[v, other + q, :, cols(k)]

        retbox[v, me, :, cols(k)] = servebox[v, me, :, cols(k)]

    def narrow(rows):
        return rows.astype(jnp.float32).reshape(near, step).astype(jnp.bfloat16)

    def combine(v, k):
        @when(inner)
        def _():
            for q in range(2):
                gather_copy(v, k, q, 1 - mine).wait_recv()
                rows = narrow(gatherbox[v, q, :, :, cols(k)])
                part = jnp.dot(far_bring[v, q, 0], rows, preferred_element_type=jnp.float32)
                part += jnp.dot(far_bring[v, q, 1], rows, preferred_element_type=jnp.float32)
                partbox[v, q, :, cols(k)] = part.astype(jnp.bfloat16)
                part_copy(v, k, q).start()

    def mix(v, k):
        ret_copy(v, k, partner, partner).wait_recv()
        rows = narrow(retbox[v, pl.ds(2 * half, 2), :, cols(k)])
        added = jnp.dot(bring_ref[v, half, 0], rows, preferred_element_type=jnp.float32)
        added += jnp.dot(bring_ref[v, half, 1], rows, preferred_element_type=jnp.float32)
        wide = state_of(v)[:, cols(k)].astype(jnp.float32) + added

        @when(k < edge)
        def _():
            for q in range(2):
                ret_copy(v, k, partner, other + q).wait_recv()
            far = narrow(retbox[v, pl.ds(other, 2), :, cols(k)])
            more = jnp.dot(bring_ref[v, 1 - half, 0], far, preferred_element_type=jnp.float32)
            more += jnp.dot(bring_ref[v, 1 - half, 1], far, preferred_element_type=jnp.float32)
            mixbox[v, :, cols(k)] = (wide + more).astype(jnp.bfloat16)

        @when(k >= edge)
        def _():
            part_copy(v, k, 0).wait_recv()
            more = partin[v, :, cols(k)].astype(jnp.float32)
            mixbox[v, :, cols(k)] = (wide + more).astype(jnp.bfloat16)

        section_copy(v, k).start()

    def far_tables(q):
        tab_copy(q).wait_recv()
        for v in range(stops):
            tab = tabbox[q, v]
            place = lax.broadcasted_iota(jnp.int32, (capacity, tok_rows), 0).astype(jnp.float32)
            chosen = [tab[j : j + 1] == place for j in range(2)]
            picks = [jnp.where(c, 1.0, 0.0) for c in chosen]
            far_pick[v, q] = jnp.concatenate(picks, axis=0).astype(jnp.bfloat16)
            brings = [jnp.where(c, tab[2 + j : 3 + j], 0.0) for j, c in enumerate(chosen)]
            brings.append(jnp.zeros((-near % tok_rows, tok_rows), jnp.float32))
            turned = jnp.concatenate(brings, axis=0).T[:, :near]
            high = turned.astype(jnp.bfloat16)
            far_bring[v, q, 0] = high
            far_bring[v, q, 1] = (turned - high.astype(jnp.float32)).astype(jnp.bfloat16)

    def each(first, end, work):
        def turn(k, carry):
            work(k)
            return carry

        lax.fori_loop(first, end, turn, 0)

    tab_copy(mine).start()
    each(0, chunks, lambda k: dispatch(0, k))

    @when(inner)
    def _():
        for q in range(2):
            far_tables(q)

    fetch_up.wait()
    passed = 0
    for v in range(stops):
        total[...] = jnp.zeros_like(total)
        square[...] = jnp.zeros_like(square)

        def take(k):
            @when(jnp.logical_and(k >= passed, k < last))
            def _():
                pass_on(v, k)

            expand(v, k)

        each(0, chunks, take)
        factor = lax.rsqrt(square[...] * (1.0 / width) + 1e-06)
        before = total[...] * factor
        hidden[...] = (before * jax.nn.sigmoid(before)).astype(jnp.bfloat16)
        if v == 0:
            fetch_down.wait()
        each(0, jnp.where(outer, chunks, early), lambda k: serve(v, k))
        each(edge, max(edge, lead), lambda k: combine(v, k))

        def turn(k):
            @when(jnp.logical_and(inner, k + early < chunks))
            def _():
                serve(v, k + early)

            @when(jnp.logical_and(k + lead >= edge, k + lead < chunks))
            def _():
                combine(v, k + lead)

            mix(v, k)
            if v < stops - 1:

                @when(k >= 1)
                def _():
                    section_copy(v, k - 1).wait_recv()
                    dispatch(v + 1, k - 1)

                @when(jnp.logical_and(k >= lag, k - lag < last))
                def _():
                    pass_on(v + 1, k - lag)

        each(0, chunks, turn)
        if v < stops - 1:
            section_copy(v, chunks - 1).wait_recv()
            dispatch(v + 1, chunks - 1)
            passed = min(chunks - lag, last)
        else:
            each(0, chunks, lambda k: section_copy(v, k).wait_recv())

    for v in range(stops):

        def drain(k):
            out_copy(v, k, partner, me).wait_send()
            ret_copy(v, k, partner, me).wait_send()
            section_copy(v, k).wait_send()

            @when(k < last)
            def _():
                cross_copy(v, k, mine).wait_send()

            @when(jnp.logical_and(inner, k < last))
            def _():
                for q in range(2):
                    forward_copy(v, k, q).wait_send()

            @when(jnp.logical_and(inner, k >= edge))
            def _():
                for q in range(2):
                    part_copy(v, k, q).wait_send()

            @when(jnp.logical_and(outer, k >= edge))
            def _():
                for q in range(2):
                    gather_copy(v, k, q, mine).wait_send()

            @when(k >= last)
            def _():
                for q in range(2):
                    out_copy(v, k, other + q, me).wait_send()

            @when(k < edge)
            def _():
                for q in range(2):
                    ret_copy(v, k, other + q, me).wait_send()

        each(0, chunks, drain)
    tab_copy(mine).wait_send()


def kernel_body(activations, routes, combine, norm_gain, up_weight, down_weight):
    state = activations[0]
    experts, sections = lax.axis_size("expert"), lax.axis_size("section")
    tok_rows, width = state.shape
    stops, chosen = routes.shape[0], routes.shape[3]
    inner = up_weight.shape[3]
    capacity = tok_rows * chosen // experts * 9 // 8
    slots, near = experts * capacity, experts // 2 * capacity
    step = 512 if width % 512 == 0 else width
    chunks = width // step
    pick, bring, tab = tables(routes[:, 0], combine[:, 0], experts, capacity)
    vmem = pl.BlockSpec(memory_space=pltpu.VMEM)
    anywhere = pl.BlockSpec(memory_space=pl.ANY)
    dma = pltpu.SemaphoreType.DMA
    half_rows = (stops, experts // 2, experts // 2, capacity, width)
    box = pltpu.VMEM((stops, experts, capacity, width), jnp.bfloat16)
    whole = pltpu.VMEM((stops, tok_rows, width), jnp.bfloat16)
    twice = pltpu.VMEM((stops, experts // 2, tok_rows, width), jnp.bfloat16)
    by_expert, by_half, line = dma((stops, experts, chunks)), dma((stops, 2, chunks)), dma((stops, chunks))
    out = pl.pallas_call(
        functools.partial(relay_kernel, stops, sections, capacity, step, 2, 4, 2, 2),
        out_shape=jax.ShapeDtypeStruct((tok_rows, width), jnp.bfloat16),
        in_specs=[vmem] * 5 + [anywhere] * 2,
        out_specs=anywhere,
        scratch_shapes=[
            pltpu.VMEM((width, inner), jnp.bfloat16),
            pltpu.VMEM((inner, width), jnp.bfloat16),
            pltpu.VMEM((max(stops - 1, 1), tok_rows, width), jnp.bfloat16),
            whole,
            box, box, box, box,
            twice,
            pltpu.VMEM(half_rows, jnp.bfloat16),
            pltpu.VMEM(half_rows, jnp.bfloat16),
            twice, whole,
            pltpu.VMEM((2, stops, 8, tok_rows), jnp.float32),
            pltpu.VMEM((stops, 2, near, tok_rows), jnp.bfloat16),
            pltpu.VMEM((stops, 2, 2, tok_rows, near), jnp.bfloat16),
            pltpu.VMEM((slots, inner), jnp.float32),
            pltpu.VMEM((slots, inner), jnp.bfloat16),
            pltpu.VMEM((slots, 1), jnp.float32),
            dma((2,)),
            by_expert, by_expert, by_expert, by_expert, line, line,
            line, by_half, by_half, by_half, by_half, by_half, line,
            dma, dma((2,)),
        ],
        compiler_params=pltpu.CompilerParams(
            collective_id=0, has_side_effects=True, vmem_limit_bytes=62 << 20
        ),
    )(state, pick, bring, tab, norm_gain, up_weight[0, 0], down_weight[0, 0])
    return out[None]


def slot_of(expert_ids, experts):
    flattened = expert_ids.reshape(-1)
    onehot = (flattened[:, None] == jnp.arange(experts, dtype=jnp.int32)[None, :]).astype(jnp.int32)
    before = jnp.cumsum(onehot, axis=0) - onehot
    return jnp.sum(before * onehot, axis=1).reshape(expert_ids.shape)


def plain_body(activations, routes, combine, norm_gain, up_weight, down_weight):
    state = activations[0]
    gain_row = norm_gain[0]
    up_proj = up_weight[0, 0]
    down_proj = down_weight[0, 0]
    experts = lax.axis_size("expert")
    tok_rows = state.shape[0]
    width = state.shape[1]
    chosen = routes.shape[3]
    capacity = tok_rows * chosen // experts * 9 // 8
    for visit in range(routes.shape[0]):
        expert_ids = routes[visit, 0]
        weights_now = combine[visit, 0]
        wide_state = state.astype(jnp.float32)
        normed = (
            wide_state
            * lax.rsqrt(jnp.mean(wide_state * wide_state, axis=-1, keepdims=True) + 1e-06)
            * gain_row
        ).astype(jnp.bfloat16)
        slots = slot_of(expert_ids, experts)
        spread = jnp.broadcast_to(normed[:, None, :], (tok_rows, chosen, width))
        outbox = (
            jnp.zeros((experts, capacity, width), jnp.bfloat16).at[expert_ids, slots].set(spread)
        )
        arrived = lax.all_to_all(outbox, "expert", split_axis=0, concat_axis=0, tiled=True)
        hidden = jax.nn.silu(
            jnp.dot(arrived.reshape(-1, width), up_proj, preferred_element_type=jnp.float32)
        ).astype(jnp.bfloat16)
        served = (
            jnp.dot(hidden, down_proj, preferred_element_type=jnp.float32)
            .astype(jnp.bfloat16)
            .reshape(arrived.shape)
        )
        returned = lax.all_to_all(served, "expert", split_axis=0, concat_axis=0, tiled=True)
        picked = returned[expert_ids, slots].astype(jnp.float32)
        mixed = (wide_state + jnp.sum(picked * weights_now[..., None], axis=1)).astype(jnp.bfloat16)
        state = from_behind(mixed, "section", 1)
    return state[None]


def body(activations, routes, combine, norm_gain, up_weight, down_weight):
    experts = lax.axis_size("expert")
    tok_rows, width = activations.shape[1:]
    stops, inner = routes.shape[0], up_weight.shape[3]
    capacity = tok_rows * routes.shape[3] // experts * 9 // 8
    boxes = 6 * stops * experts * capacity * width * 2
    rest = 4 * width * inner + (7 * stops + 1) * tok_rows * width * 2 + experts * capacity * inner * 6
    fits = experts == 4 and boxes + rest <= VMEM_ROOM
    run = kernel_body if fits else plain_body
    return run(activations, routes, combine, norm_gain, up_weight, down_weight)


def solution(mesh):
    placed = (
        P("section", ("dp", "expert"), None),
        P(None, "section", ("dp", "expert"), None),
        P(None, "section", ("dp", "expert"), None),
        P("section", None),
        P("section", "expert", None, None),
        P("section", "expert", None, None),
    )
    return jax.shard_map(
        body,
        mesh=mesh,
        in_specs=placed,
        out_specs=P("section", ("dp", "expert"), None),
        check_vma=False,
    )
```
